32 devices in a mesh: ctx: 8 (over z, x), head: 4 (over y, core).
Axes of the slice: x: 2, y: 2, z: 4, core: 2. Of those that a mesh axis runs over, the one named last changes fastest.
Arguments:
- query_rows: bfloat16 [8192, 6144], P(('ctx', 'head')), may hold values from -0.52734375 to 0.52734375
- key_rows: bfloat16 [8192, 6144], P(('ctx', 'head')), may hold values from -0.52734375 to 0.52734375
- value_rows: bfloat16 [8192, 6144], P(('ctx', 'head')), may hold values from -0.62890625 to 0.62890625
- grad_out: bfloat16 [8192, 6144], P(('ctx', 'head')), may hold values from -0.62890625 to 0.62890625
- decay_rates: float32 [48], replicated, as said below
Outputs:
- query_gradient: bfloat16 [8192, 6144], P(('ctx', 'head'))
- grad_key: bfloat16 [8192, 6144], P(('ctx', 'head'))
- value_gradient: bfloat16 [8192, 6144], P(('ctx', 'head'))
The draws below stay inside these ranges and needn't reach their ends.
Inputs may be any that keep to these rules, and one draw needn't show every extreme that they name: decay_rates lie between 0.1 / 8192 and 24 / 256.
All inputs are finite; a program needn't handle non-finite values.
Results may differ from the reference program's by a relative error of at most 0.0056.
Values may be sent and summed in bfloat16 or wider, within the bound.
No kernel may reach another device: no remote copies, remote signals or barrier semaphores. Data moves between devices by JAX's collectives and lax.ppermute only.
A program may use at most 128 MiB of HBM per device.

```python
import jax
import jax.numpy as jnp
from jax import lax

HEADS = 48
DH = 128
BLOCK = 256
TOKENS = 8192


def draw_decay_rates(key, part):
    pick_key, slow_key, fast_key = jax.random.split(key, 3)
    order = jax.random.permutation(pick_key, HEADS)
    slow_low = 0.1 / TOKENS
    slow_high = 2.0 / TOKENS
    fast_low = 12.0 / BLOCK
    fast_high = 24.0 / BLOCK
    slow = jnp.exp(jax.random.uniform(slow_key, (HEADS,), jnp.float32, jnp.log(slow_low), jnp.log(slow_high)))
    fast = jnp.exp(jax.random.uniform(fast_key, (HEADS,), jnp.float32, jnp.log(fast_low), jnp.log(fast_high)))
    fast_heads = order < HEADS // 2
    return jnp.where(fast_heads, fast, slow).astype(jnp.float32)


def shard_levels(key, extent, shards, low, top_value):
    loudness, own = 1.0, jax.random.fold_in(key, 6)
    for dim, shards_of in shards:
        heights = jnp.exp(jax.random.uniform(jax.random.fold_in(own, dim), (shards_of,), jnp.float32, low / len(shards), top_value / len(shards)))
        loudness = loudness * jnp.repeat(heights, extent[dim] // shards_of).reshape([-1 if axis == dim else 1 for axis in range(len(extent))])
    return loudness


def gaussian(own_key, shape, width, most, shards=(), kind=jnp.bfloat16):
    loudness = shard_levels(own_key, shape, shards, -0.22, 0.18) if shards else 1.0
    values = jax.random.normal(own_key, shape, jnp.float32) * width * loudness
    return jnp.minimum(jnp.maximum(values, -most), most).astype(kind)


def setup_inputs(seed: int = 0) -> dict:
    splits = jax.random.split(jax.random.key(seed), 6)
    return {
        "query_rows": gaussian(splits[0], (TOKENS, HEADS * DH), (DH ** -0.5), 0.52734375, ((0, 32),)),
        "key_rows": gaussian(splits[1], (TOKENS, HEADS * DH), (DH ** -0.5), 0.52734375, ((0, 32),)),
        "value_rows": gaussian(splits[2], (TOKENS, HEADS * DH), (TOKENS ** -0.25), 0.62890625, ((0, 32),)),
        "grad_out": gaussian(splits[3], (TOKENS, HEADS * DH), (TOKENS ** -0.25), 0.62890625, ((0, 32),)),
        "decay_rates": draw_decay_rates(jax.random.fold_in(splits[5], 71), 0),
    }


def round_keep(values):
    return lax.optimization_barrier(values.astype(jnp.bfloat16)).astype(jnp.float32)


def one_head(query_col, key_col, value_col, grad_col, rate):
    nblocks = TOKENS // BLOCK
    q_blocks = query_col.astype(jnp.float32).reshape(nblocks, BLOCK, DH)
    key_block_list = key_col.astype(jnp.float32).reshape(nblocks, BLOCK, DH)
    v_blocks = value_col.astype(jnp.float32).reshape(nblocks, BLOCK, DH)
    gradient_block_list = grad_col.astype(jnp.float32).reshape(nblocks, BLOCK, DH)
    position = jnp.arange(BLOCK, dtype=jnp.float32)
    offset = position[:, None] - position[None, :]
    decay_mask = jnp.where(offset >= 0.0, jnp.exp(-rate * jnp.maximum(offset, 0.0)), 0.0)
    weight_gradient_set = round_keep(jnp.einsum('nid,njd->nij', gradient_block_list, v_blocks) * decay_mask[None])
    forward_weight_set = round_keep(jnp.einsum('nid,njd->nij', q_blocks, key_block_list) * decay_mask[None])
    keys_decayed = round_keep(key_block_list * jnp.exp(-rate * (BLOCK - 1.0 - position))[None, :, None])
    decayed_query_rows = round_keep(q_blocks * jnp.exp(-rate * position)[None, :, None])
    block_kv = jnp.einsum('njd,nje->nde', keys_decayed, v_blocks)
    query_decay_block = jnp.einsum('ubh,uby->uhy', decayed_query_rows, gradient_block_list)
    span = jnp.exp(-rate * BLOCK)

    def advance(state, term):
        return span * state + term, state

    start = jnp.zeros((DH, DH), jnp.float32)
    _, state_before = lax.scan(advance, start, block_kv)
    _, state_after = lax.scan(advance, start, query_decay_block, reverse=True)
    state_before_bfloat = round_keep(state_before)
    state_after_bfloat = round_keep(state_after)
    leading_part = jnp.exp(-rate * (position + 1.0))[None, :, None]
    trailing_part = jnp.exp(-rate * (BLOCK - position))[None, :, None]
    query_gradient = jnp.einsum('ytb,ybr->ytr', weight_gradient_set, key_block_list) + leading_part * jnp.einsum('kzu,kpu->kzp', gradient_block_list, state_before_bfloat)
    grad_key = jnp.einsum('nij,nid->njd', weight_gradient_set, q_blocks) + trailing_part * jnp.einsum('nje,nde->njd', v_blocks, state_after_bfloat)
    value_gradient = jnp.einsum('lov,lox->lvx', forward_weight_set, gradient_block_list) + trailing_part * jnp.einsum('cxk,ckh->cxh', key_block_list, state_after_bfloat)
    return (query_gradient.reshape(TOKENS, DH).astype(jnp.bfloat16),
            grad_key.reshape(TOKENS, DH).astype(jnp.bfloat16),
            value_gradient.reshape(TOKENS, DH).astype(jnp.bfloat16))


def reference(query_rows, key_rows, value_rows, grad_out, decay_rates):
    def per_head(index):
        first = (index * DH).astype(jnp.int32)
        return one_head(lax.dynamic_slice_in_dim(query_rows, first, DH, 1),
                        lax.dynamic_slice_in_dim(key_rows, first, DH, 1),
                        lax.dynamic_slice_in_dim(value_rows, first, DH, 1),
                        lax.dynamic_slice_in_dim(grad_out, first, DH, 1),
                        decay_rates[index])

    query_gradient, grad_key, value_gradient = lax.map(per_head, jnp.arange(HEADS, dtype=jnp.int32))

    def regroup(stacked):
        return jnp.transpose(stacked, (1, 0, 2)).reshape(TOKENS, HEADS * DH)

    return (regroup(query_gradient), regroup(grad_key), regroup(value_gradient))
```

```python
import functools

import jax
import jax.numpy as jnp
from jax import lax
from jax.experimental import pallas as pl
from jax.experimental.pallas import tpu as pltpu
from jax.sharding import PartitionSpec as P

DH = 128
AXES = ("ctx", "head")
CHUNKS = 2

F32 = jnp.float32
BF16 = jnp.bfloat16


def dot(a, b, contract):
    return lax.dot_general(a, b, ((contract[:1], contract[1:]), ((), ())), preferred_element_type=F32)


def splat(rate, count):
    return jnp.exp(jnp.full((8, DH), -rate * count, F32))


def scaled(weight, state):
    return (state.astype(F32).reshape(DH // 8, 8, DH) * weight[None]).reshape(DH, DH)


def place(shape):
    ctx, head = lax.axis_index("ctx"), lax.axis_index("head")
    ys = shape["head"] // 2
    return head % 2, (ctx % 2) * ys + head // 2, ctx // 2


def exchange(value, shape, level, flip):
    ys = shape["head"] // 2
    pairs = []
    for source in range(shape["ctx"] * shape["head"]):
        ctx, head = divmod(source, shape["head"])
        core, member, z = head % 2, (ctx % 2) * ys + head // 2, ctx // 2
        if level == "core":
            core ^= flip
        elif level == "group":
            member ^= flip
        else:
            z ^= flip
        target = ((z * 2 + member // ys) * ys + member % ys) * 2 + core
        pairs.append((source, target))
    return lax.ppermute(value, AXES, pairs)


def block_states(shape, first, count, per_step, mine, dtype, query, key, value, grad, rates):
    rows = query.shape[0]

    def first_head():
        core = place(shape)[0]
        return first + (core if mine else 1 - core) * count

    def body(rates_ref, q_ref, k_ref, v_ref, g_ref, out_ref):
        base = first_head() + pl.program_id(0) * per_step
        position = lax.broadcasted_iota(jnp.int32, (1, rows), 1).astype(F32)
        for i in range(per_step):
            rate = rates_ref[base + i]
            columns = slice(i * DH, (i + 1) * DH)
            key_decay = jnp.exp(-rate * (rows - 1.0 - position))
            query_decay = jnp.exp(-rate * position)
            keys = (k_ref[:, columns].T.astype(F32) * key_decay).astype(BF16)
            queries = (q_ref[:, columns].T.astype(F32) * query_decay).astype(BF16)
            out_ref[0, i] = dot(keys, v_ref[:, columns], (1, 0)).astype(dtype)
            out_ref[1, i] = dot(queries, g_ref[:, columns], (1, 0)).astype(dtype)

    rows_spec = pl.BlockSpec((rows, per_step * DH), lambda s: (0, first_head() // per_step + s))
    return pl.pallas_call(
        body,
        grid=(count // per_step,),
        in_specs=[pl.BlockSpec(memory_space=pltpu.SMEM)] + [rows_spec] * 4,
        out_specs=pl.BlockSpec((2, per_step, DH, DH), lambda s: (0, s, 0, 0)),
        out_shape=jax.ShapeDtypeStruct((2, count, DH, DH), dtype),
        cost_estimate=pl.CostEstimate(
            flops=count * 4 * rows * DH * DH, bytes_accessed=count * rows * DH * 8, transcendentals=0
        ),
        name="block_states",
    )(rates, query, key, value, grad)


def whole_call(body, name, outs, *args):
    vmem = pl.BlockSpec(memory_space=pltpu.VMEM)
    size = sum(a.size * a.dtype.itemsize for a in args) + sum(o.size * o.dtype.itemsize for o in outs)
    return pl.pallas_call(
        body,
        in_specs=[pl.BlockSpec(memory_space=pltpu.SMEM)] + [vmem] * (len(args) - 1),
        out_specs=[vmem] * len(outs),
        out_shape=outs,
        cost_estimate=pl.CostEstimate(flops=size, bytes_accessed=size, transcendentals=0),
        name=name,
    )(*args)


def states(heads, dtype, lead=(2,)):
    return jax.ShapeDtypeStruct((*lead, heads, DH, DH), dtype)


def chip_totals(shape, rows, first, count, group, per, rates, own, other):
    def body(rates_ref, own_ref, other_ref, keep_ref, *send_refs):
        core, member, _ = place(shape)
        base = first + core * count
        for flip in range(group):
            start = (member ^ flip) * per
            for i in range(per):
                rate = rates_ref[base + start + i]
                early = splat(rate, rows * (1 - core).astype(F32))
                late = splat(rate, rows * core.astype(F32))
                total = scaled(early, own_ref[0, start + i]) + scaled(late, other_ref[0, start + i])
                after = scaled(late, own_ref[1, start + i]) + scaled(early, other_ref[1, start + i])
                out = keep_ref if flip == 0 else send_refs[flip - 1]
                out[0, i] = total.astype(out.dtype)
                out[1, i] = after.astype(out.dtype)

    outs = [states(per, F32)] + [states(per, BF16)] * (group - 1)
    return whole_call(body, "chip_totals", outs, rates, own, other)


def group_totals(shape, rows, first, count, group, per, bits, rates, keep, others):
    def body(rates_ref, keep_ref, *refs):
        other_refs, send_refs = refs[: group - 1], refs[group - 1 :]
        core, member, z = place(shape)
        base = first + core * count + member * per
        for i in range(per):
            rate = rates_ref[base + i]
            total = after = jnp.zeros((DH, DH), F32)
            for flip in range(group):
                ref = keep_ref if flip == 0 else other_refs[flip - 1]
                where = member ^ flip
                total += scaled(splat(rate, 2.0 * rows * (group - 1 - where).astype(F32)), ref[0, i])
                after += scaled(splat(rate, 2.0 * rows * where.astype(F32)), ref[1, i])
            for bit in range(bits):
                lower = (z >> bit) % 2 == 0
                send_refs[bit][i] = jnp.where(lower, total, after).astype(BF16)

    return whole_call(body, "group_totals", [states(per, BF16, ())] * bits, rates, keep, *others)


def group_carries(shape, rows, first, count, group, per, depth, rates, keep, others, zs):
    def body(rates_ref, keep_ref, *refs):
        other_refs, z_refs = refs[: group - 1], refs[group - 1 : group + depth - 2]
        own_ref, *send_refs = refs[group + depth - 2 :]
        core, member, z = place(shape)
        base = first + core * count + member * per

        def weight(rate, span, steps):
            kept = jnp.where(steps >= 0, 1.0, 0.0)
            return splat(rate, span * jnp.maximum(steps, 0).astype(F32)) * kept

        for i in range(per):
            rate = rates_ref[base + i]
            before = after = jnp.zeros((DH, DH), F32)
            for flip in range(1, depth):
                where = z ^ flip
                before += scaled(weight(rate, 2.0 * group * rows, z - 1 - where), z_refs[flip - 1][i])
                after += scaled(weight(rate, 2.0 * group * rows, where - z - 1), z_refs[flip - 1][i])
            for target in range(group):
                at = member ^ target
                here = scaled(splat(rate, 2.0 * rows * at.astype(F32)), before)
                there = scaled(splat(rate, 2.0 * rows * (group - 1 - at).astype(F32)), after)
                for flip in range(group):
                    ref = keep_ref if flip == 0 else other_refs[flip - 1]
                    where = member ^ flip
                    here += scaled(weight(rate, 2.0 * rows, at - 1 - where), ref[0, i])
                    there += scaled(weight(rate, 2.0 * rows, where - at - 1), ref[1, i])
                out = own_ref if target == 0 else send_refs[target - 1]
                out[0, i] = here.astype(out.dtype)
                out[1, i] = there.astype(out.dtype)

    outs = [states(per, F32)] + [states(per, BF16)] * (group - 1)
    return whole_call(body, "group_carries", outs, rates, keep, *others, *zs)


def device_carries(shape, rows, first, count, group, per, rates, own, other, carries):
    def body(rates_ref, own_ref, other_ref, *refs):
        carry_refs, (mine_ref, send_ref) = refs[:group], refs[group:]
        core, member, _ = place(shape)
        base = first + core * count
        zero_first = (core == 0).astype(F32)
        for flip in range(group):
            start = (member ^ flip) * per
            for i in range(per):
                at = start + i
                rate = rates_ref[base + at]
                before = carry_refs[flip][0, i].astype(F32)
                after = carry_refs[flip][1, i].astype(F32)
                early = splat(rate, rows * (1.0 - zero_first))
                late = splat(rate, rows * zero_first)
                mine_ref[0, at] = (scaled(early, before) + (1.0 - zero_first) * other_ref[0, at].astype(F32)).astype(BF16)
                mine_ref[1, at] = (scaled(late, after) + zero_first * other_ref[1, at].astype(F32)).astype(BF16)
                send_ref[0, at] = (scaled(late, before) + zero_first * own_ref[0, at].astype(F32)).astype(BF16)
                send_ref[1, at] = (scaled(early, after) + (1.0 - zero_first) * own_ref[1, at].astype(F32)).astype(BF16)

    return whole_call(body, "device_carries", [states(count, BF16)] * 2, rates, own, other, *carries)


def sublane_powers(rate, rows, sign):
    position = lax.broadcasted_iota(jnp.int32, (8, DH), 0).astype(F32)
    powers = jnp.exp(sign * rate * position)
    size = 8
    while size < rows:
        powers = jnp.concatenate([powers, jnp.tile(splat(rate, -sign * size), (size // 8, 1)) * powers], axis=0)
        size *= 2
    return powers


def gradients(shape, first, count, per_step, mine, query, key, value, grad, rates, carries, previous):
    rows = query.shape[0]

    def first_head():
        core = place(shape)[0]
        return first + (core if mine else 1 - core) * count

    def body(rates_ref, q_ref, k_ref, v_ref, g_ref, carry_ref, *refs):
        gq_ref, gk_ref, gv_ref = refs[-3:]
        base = first_head() + pl.program_id(0) * per_step
        lane = lax.broadcasted_iota(jnp.int32, (1, rows), 1).astype(F32)
        row_index = lax.broadcasted_iota(jnp.int32, (rows, rows), 0)
        column_index = lax.broadcasted_iota(jnp.int32, (rows, rows), 1)
        reach = rows // DH
        for i in range(per_step):
            rate = rates_ref[base + i]
            columns = slice(i * DH, (i + 1) * DH)
            q, k, v, g = (ref[:, columns] for ref in (q_ref, k_ref, v_ref, g_ref))
            falling, rising = (sublane_powers(rate, rows, sign) for sign in (-1.0, 1.0))
            falling_lane, rising_lane = jnp.exp(-rate * lane), jnp.exp(rate * lane)
            lower = jnp.where(
                row_index >= column_index, jnp.tile(falling, (1, reach)) * rising_lane, 0.0
            )
            upper = jnp.where(
                row_index <= column_index, jnp.tile(rising, (1, reach)) * falling_lane, 0.0
            )
            weights = (dot(g, v, (1, 1)) * lower).astype(BF16)
            weights_back = (dot(v, g, (1, 1)) * upper).astype(BF16)
            forward_back = (dot(k, q, (1, 1)) * upper).astype(BF16)
            before, after = carry_ref[0, i], carry_ref[1, i]
            leading = falling * jnp.tile(splat(rate, 1.0), (rows // 8, 1))
            trailing = rising * jnp.tile(splat(rate, float(rows)), (rows // 8, 1))
            gq_ref[:, columns] = (dot(weights, k, (1, 0)) + leading * dot(g, before, (1, 1))).astype(BF16)
            gk_ref[:, columns] = (dot(weights_back, q, (1, 0)) + trailing * dot(v, after, (1, 1))).astype(BF16)
            gv_ref[:, columns] = (dot(forward_back, g, (1, 0)) + trailing * dot(k, after, (1, 0))).astype(BF16)

    rows_spec = pl.BlockSpec((rows, per_step * DH), lambda s: (0, first_head() // per_step + s))
    out = jax.ShapeDtypeStruct(query.shape, BF16)
    return pl.pallas_call(
        body,
        grid=(count // per_step,),
        in_specs=[pl.BlockSpec(memory_space=pltpu.SMEM)]
        + [rows_spec] * 4
        + [pl.BlockSpec((2, per_step, DH, DH), lambda s: (0, s, 0, 0))]
        + [pl.BlockSpec(memory_space=pl.ANY)] * len(previous),
        out_specs=[rows_spec] * 3,
        out_shape=[out] * 3,
        input_output_aliases={6 + i: i for i in range(len(previous))},
        cost_estimate=pl.CostEstimate(
            flops=count * 12 * rows * rows * DH, bytes_accessed=count * rows * DH * 14, transcendentals=0
        ),
        name="gradients",
    )(rates, query, key, value, grad, carries, *previous)


def steps_of(count, first):
    return next(n for n in (4, 3, 2, 1) if count % n == 0 and first % n == 0)


def local(shape, query, key, value, grad, rates):
    rows = query.shape[0]
    heads = query.shape[1] // DH
    group = shape["head"]
    depth = shape["ctx"] // 2
    bits = (depth - 1).bit_length()
    units = heads // (2 * group)
    sizes = [(units + CHUNKS - 1 - n) // CHUNKS for n in range(CHUNKS)]
    chunks, first = [], 0
    for per in sizes:
        if per:
            chunks.append((first, per * group, per))
            first += 2 * per * group
    arrays = (query, key, value, grad, rates)

    def totals(chunk):
        first, count, per = chunk
        step = steps_of(count, first)
        send = block_states(shape, first, count, step, False, BF16, *arrays)
        other = exchange(send, shape, "core", 1)
        own = block_states(shape, first, count, step, True, F32, *arrays)
        keep, *sends = chip_totals(shape, rows, first, count, group, per, rates, own, other)
        others = [exchange(s, shape, "group", f + 1) for f, s in enumerate(sends)]
        return own, other, keep, others

    def carried(chunk, kept):
        first, count, per = chunk
        own, other, keep, others = kept
        sends = group_totals(shape, rows, first, count, group, per, bits, rates, keep, others)
        zs = [exchange(sends[f.bit_length() - 1], shape, "z", f) for f in range(1, depth)]
        mine, *sends = group_carries(shape, rows, first, count, group, per, depth, rates, keep, others, zs)
        carries = [mine] + [exchange(s, shape, "group", f + 1) for f, s in enumerate(sends)]
        state, send = device_carries(shape, rows, first, count, group, per, rates, own, other, carries)
        return state, exchange(send, shape, "core", 1)

    kept = [totals(chunk) for chunk in chunks]
    outs = ()
    for chunk, keep in zip(chunks, kept):
        first, count, per = chunk
        step = steps_of(count, first)
        state, other_state = carried(chunk, keep)
        outs = gradients(shape, first, count, step, True, *arrays, state, outs)
        outs = gradients(shape, first, count, step, False, *arrays, other_state, outs)
    return tuple(outs)


def solution(mesh):
    split = P(AXES, None)
    return jax.shard_map(
        functools.partial(local, dict(mesh.shape)),
        mesh=mesh,
        in_specs=(split, split, split, split, P()),
        out_specs=(split, split, split),
        check_vma=False,
    )
```

```python
import functools

import jax
import jax.numpy as jnp
from jax import lax
from jax.experimental import pallas as pl
from jax.experimental.pallas import tpu as pltpu
from jax.sharding import PartitionSpec as P

DH = 128
AXES = ("ctx", "head")
CHUNKS = 2

F32 = jnp.float32
BF16 = jnp.bfloat16


def dot(a, b, contract):
    return lax.dot_general(a, b, ((contract[:1], contract[1:]), ((), ())), preferred_element_type=F32)


def splat(rate, count):
    return jnp.exp(jnp.full((8, DH), -rate * count, F32))


def scaled(weight, state):
    return (state.astype(F32).reshape(DH // 8, 8, DH) * weight[None]).reshape(DH, DH)


def place(shape):
    ctx, head = lax.axis_index("ctx"), lax.axis_index("head")
    ys = shape["head"] // 2
    return head % 2, (ctx % 2) * ys + head // 2, ctx // 2


def exchange(value, shape, level, flip):
    ys = shape["head"] // 2
    pairs = []
    for source in range(shape["ctx"] * shape["head"]):
        ctx, head = divmod(source, shape["head"])
        core, member, z = head % 2, (ctx % 2) * ys + head // 2, ctx // 2
        if level == "core":
            core ^= flip
        elif level == "group":
            member ^= flip
        else:
            z ^= flip
        target = ((z * 2 + member // ys) * ys + member % ys) * 2 + core
        pairs.append((source, target))
    return lax.ppermute(value, AXES, pairs)


def first_head(shape, first, count, mine):
    core = place(shape)[0]
    return first + (core if mine else 1 - core) * count


def after(value, *done):
    return lax.optimization_barrier((value, done))[0]


def block_states(shape, first, count, per_step, mine, dtype, rates, *arrays):
    rows = arrays[0].shape[0]
    steps = count // per_step
    width = per_step * DH

    def body(rates_ref, *refs):
        sources, staged, out_ref, sems = refs[:4], refs[4:8], refs[8], refs[9]
        base = first_head(shape, first, count, mine)
        copies = []
        for s in range(steps):
            start = pl.multiple_of((base + s * per_step) * DH, DH)
            copies.append([
                pltpu.make_async_copy(
                    source.at[:, pl.ds(start, width)], stage.at[:, pl.ds(s * width, width)], sems.at[s, n]
                )
                for n, (source, stage) in enumerate(zip(sources, staged))
            ])
        for group in copies:
            for copy in group:
                copy.start()
        position = lax.broadcasted_iota(jnp.int32, (1, rows), 1).astype(F32)
        q_ref, k_ref, v_ref, g_ref = staged
        for s in range(steps):
            for copy in copies[s]:
                copy.wait()
            for i in range(s * per_step, (s + 1) * per_step):
                rate = rates_ref[base + i]
                columns = slice(i * DH, (i + 1) * DH)
                key_decay = jnp.exp(-rate * (rows - 1.0 - position))
                query_decay = jnp.exp(-rate * position)
                keys = (k_ref[:, columns].T.astype(F32) * key_decay).astype(BF16)
                queries = (q_ref[:, columns].T.astype(F32) * query_decay).astype(BF16)
                out_ref[0, i] = dot(keys, v_ref[:, columns], (1, 0)).astype(dtype)
                out_ref[1, i] = dot(queries, g_ref[:, columns], (1, 0)).astype(dtype)

    vmem = pl.BlockSpec(memory_space=pltpu.VMEM)
    out = pl.pallas_call(
        body,
        in_specs=[pl.BlockSpec(memory_space=pltpu.SMEM)] + [pl.BlockSpec(memory_space=pltpu.HBM)] * 4,
        out_specs=[vmem] * 5,
        out_shape=[jax.ShapeDtypeStruct((rows, count * DH), BF16)] * 4 + [states(count, dtype)],
        scratch_shapes=[pltpu.SemaphoreType.DMA((steps, 4))],
        cost_estimate=pl.CostEstimate(
            flops=count * 4 * rows * DH * DH, bytes_accessed=count * rows * DH * 8, transcendentals=0
        ),
        compiler_params=pltpu.CompilerParams(vmem_limit_bytes=8 << 20),
        name="block_states",
    )(rates, *arrays)
    return out[:4], out[4]


def whole_call(body, name, outs, *args, flops=0, scratch=()):
    vmem = pl.BlockSpec(memory_space=pltpu.VMEM)
    size = sum(a.size * a.dtype.itemsize for a in args) + sum(o.size * o.dtype.itemsize for o in outs)
    return pl.pallas_call(
        body,
        in_specs=[pl.BlockSpec(memory_space=pltpu.SMEM)] + [vmem] * (len(args) - 1),
        out_specs=[vmem] * len(outs),
        out_shape=outs,
        scratch_shapes=scratch,
        cost_estimate=pl.CostEstimate(flops=flops, bytes_accessed=size, transcendentals=0),
        compiler_params=pltpu.CompilerParams(vmem_limit_bytes=8 << 20),
        name=name,
    )(*args)


def states(heads, dtype, lead=(2,)):
    return jax.ShapeDtypeStruct((*lead, heads, DH, DH), dtype)


def chip_totals(shape, rows, first, count, group, per, rates, own, other):
    def body(rates_ref, own_ref, other_ref, keep_ref, *send_refs):
        core, member, _ = place(shape)
        base = first + core * count
        for flip in range(group):
            start = (member ^ flip) * per
            for i in range(per):
                rate = rates_ref[base + start + i]
                early = splat(rate, rows * (1 - core).astype(F32))
                late = splat(rate, rows * core.astype(F32))
                total = scaled(early, own_ref[0, start + i]) + scaled(late, other_ref[0, start + i])
                after = scaled(late, own_ref[1, start + i]) + scaled(early, other_ref[1, start + i])
                out = keep_ref if flip == 0 else send_refs[flip - 1]
                out[0, i] = total.astype(out.dtype)
                out[1, i] = after.astype(out.dtype)

    outs = [states(per, F32)] + [states(per, BF16)] * (group - 1)
    return whole_call(body, "chip_totals", outs, rates, own, other)


def group_totals(shape, rows, first, count, group, per, bits, rates, keep, others):
    def body(rates_ref, keep_ref, *refs):
        other_refs, send_refs = refs[: group - 1], refs[group - 1 :]
        core, member, z = place(shape)
        base = first + core * count + member * per
        for i in range(per):
            rate = rates_ref[base + i]
            total = after = jnp.zeros((DH, DH), F32)
            for flip in range(group):
                ref = keep_ref if flip == 0 else other_refs[flip - 1]
                where = member ^ flip
                total += scaled(splat(rate, 2.0 * rows * (group - 1 - where).astype(F32)), ref[0, i])
                after += scaled(splat(rate, 2.0 * rows * where.astype(F32)), ref[1, i])
            for bit in range(bits):
                lower = (z >> bit) % 2 == 0
                send_refs[bit][i] = jnp.where(lower, total, after).astype(BF16)

    return whole_call(body, "group_totals", [states(per, BF16, ())] * bits, rates, keep, *others)


def group_carries(shape, rows, first, count, group, per, depth, rates, keep, others, zs):
    def body(rates_ref, keep_ref, *refs):
        other_refs, z_refs = refs[: group - 1], refs[group - 1 : group + depth - 2]
        own_ref, *send_refs = refs[group + depth - 2 :]
        core, member, z = place(shape)
        base = first + core * count + member * per

        def weight(rate, span, steps):
            kept = jnp.where(steps >= 0, 1.0, 0.0)
            return splat(rate, span * jnp.maximum(steps, 0).astype(F32)) * kept

        for i in range(per):
            rate = rates_ref[base + i]
            before = after = jnp.zeros((DH, DH), F32)
            for flip in range(1, depth):
                where = z ^ flip
                before += scaled(weight(rate, 2.0 * group * rows, z - 1 - where), z_refs[flip - 1][i])
                after += scaled(weight(rate, 2.0 * group * rows, where - z - 1), z_refs[flip - 1][i])
            for target in range(group):
                at = member ^ target
                here = scaled(splat(rate, 2.0 * rows * at.astype(F32)), before)
                there = scaled(splat(rate, 2.0 * rows * (group - 1 - at).astype(F32)), after)
                for flip in range(group):
                    ref = keep_ref if flip == 0 else other_refs[flip - 1]
                    where = member ^ flip
                    here += scaled(weight(rate, 2.0 * rows, at - 1 - where), ref[0, i])
                    there += scaled(weight(rate, 2.0 * rows, where - at - 1), ref[1, i])
                out = own_ref if target == 0 else send_refs[target - 1]
                out[0, i] = here.astype(out.dtype)
                out[1, i] = there.astype(out.dtype)

    outs = [states(per, F32)] + [states(per, BF16)] * (group - 1)
    return whole_call(body, "group_carries", outs, rates, keep, *others, *zs)


def device_carries(shape, rows, first, count, group, per, rates, own, other, carries):
    def body(rates_ref, own_ref, other_ref, *refs):
        carry_refs, (mine_ref, send_ref) = refs[:group], refs[group:]
        core, member, _ = place(shape)
        base = first + core * count
        zero_first = (core == 0).astype(F32)
        for flip in range(group):
            start = (member ^ flip) * per
            for i in range(per):
                at = start + i
                rate = rates_ref[base + at]
                before = carry_refs[flip][0, i].astype(F32)
                after = carry_refs[flip][1, i].astype(F32)
                early = splat(rate, rows * (1.0 - zero_first))
                late = splat(rate, rows * zero_first)
                mine_ref[0, at] = (scaled(early, before) + (1.0 - zero_first) * other_ref[0, at].astype(F32)).astype(BF16)
                mine_ref[1, at] = (scaled(late, after) + zero_first * other_ref[1, at].astype(F32)).astype(BF16)
                send_ref[0, at] = (scaled(late, before) + zero_first * own_ref[0, at].astype(F32)).astype(BF16)
                send_ref[1, at] = (scaled(early, after) + (1.0 - zero_first) * own_ref[1, at].astype(F32)).astype(BF16)

    return whole_call(body, "device_carries", [states(count, BF16)] * 2, rates, own, other, *carries)


def sublane_powers(rate, rows, sign):
    position = lax.broadcasted_iota(jnp.int32, (8, DH), 0).astype(F32)
    powers = jnp.exp(sign * rate * position)
    size = 8
    while size < rows:
        powers = jnp.concatenate([powers, jnp.tile(splat(rate, -sign * size), (size // 8, 1)) * powers], axis=0)
        size *= 2
    return powers


def within_block(shape, first, count, mine, rates, staged):
    rows = staged[0].shape[0]
    blocks = rows // DH
    spans = [(slice(a * DH, (a + 1) * DH), slice(a * DH, rows)) for a in range(blocks)]

    def weigh(rate, q, k, v, g, held):
        lane = lax.broadcasted_iota(jnp.int32, (1, DH), 1).astype(F32)
        row_index = lax.broadcasted_iota(jnp.int32, (DH, DH), 0)
        column_index = lax.broadcasted_iota(jnp.int32, (DH, DH), 1)
        full = sublane_powers(rate, DH, 1.0) * jnp.exp(-rate * lane)
        masks = [jnp.where(row_index <= column_index, full, 0.0)]
        for n in range(1, blocks):
            masks.append(full * jnp.tile(splat(rate, float(n * DH)), (DH // 8, 1)))
        for a, (here, rest) in enumerate(spans):
            mask = jnp.concatenate(masks[: blocks - a], axis=1)
            held[0, here, rest] = (dot(v[here], g[rest], (1, 1)) * mask).astype(BF16)
            held[1, here, rest] = (dot(k[here], q[rest], (1, 1)) * mask).astype(BF16)

    def apply(q, k, g, held, put):
        for b, (here, rest) in enumerate(spans):
            put(1, here, dot(held[0, here, rest], q[rest], (1, 0)))
            put(2, here, dot(held[1, here, rest], g[rest], (1, 0)))
            pieces = [held[0, spans[a][0], here].T for a in range(b + 1)]
            put(0, here, dot(jnp.concatenate(pieces, axis=1), k[: (b + 1) * DH], (1, 0)))

    def body(rates_ref, q_ref, k_ref, v_ref, g_ref, out_ref, *held):
        base = first_head(shape, first, count, mine)

        def columns(head):
            return pl.ds(pl.multiple_of(head * DH, DH), DH)

        def weigh_head(head, slot):
            weigh(rates_ref[base + head], *(ref.at[:, columns(head)] for ref in (q_ref, k_ref, v_ref, g_ref)), held[slot])

        def apply_head(head, slot):
            def put(n, here, block):
                out_ref[n, here, columns(head)] = block

            apply(*(ref.at[:, columns(head)] for ref in (q_ref, k_ref, g_ref)), held[slot], put)

        weigh_head(0, 0)

        def step(s, carry):
            weigh_head(2 * s + 1, 1)
            apply_head(2 * s, 0)
            weigh_head(jnp.minimum(2 * s + 2, count - 1), 0)
            apply_head(2 * s + 1, 1)
            return carry

        lax.fori_loop(0, count // 2, step, 0)

    return whole_call(
        body, "within_block", [jax.ShapeDtypeStruct((3, rows, count * DH), F32)], rates, *staged,
        flops=count * 13 * rows * rows * DH // 2, scratch=[pltpu.VMEM((2, rows, rows), BF16)] * 2,
    )[0]


def across_blocks(shape, first, count, mine, width, rates, staged, inside, carries, previous):
    rows = staged[0].shape[0]
    together = 2 if count % 2 == 0 else 1
    steps = count // together

    def diagonal(pair):
        if len(pair) == 1:
            return pair[0]
        zero = jnp.zeros((DH, DH), BF16)
        return jnp.concatenate(
            [jnp.concatenate([pair[0], zero], axis=1), jnp.concatenate([zero, pair[1]], axis=1)], axis=0
        )

    def body(rates_ref, k_ref, v_ref, g_ref, inside_ref, carry_ref, *refs):
        outs, scratch, sems = refs[-5:-2], refs[-2], refs[-1]
        base = first_head(shape, first, count, mine)
        copies = []
        for s in range(steps):
            heads = range(s * together, (s + 1) * together)
            columns = slice(s * together * DH, (s + 1) * together * DH)
            rates_here = [rates_ref[base + h] for h in heads]
            leading = jnp.concatenate(
                [sublane_powers(r, rows, -1.0) * jnp.tile(splat(r, 1.0), (rows // 8, 1)) for r in rates_here], axis=1
            )
            trailing = jnp.concatenate(
                [sublane_powers(r, rows, 1.0) * jnp.tile(splat(r, float(rows)), (rows // 8, 1)) for r in rates_here],
                axis=1,
            )
            before = diagonal([carry_ref[0, h] for h in heads])
            later = diagonal([carry_ref[1, h] for h in heads])
            parts = (
                leading * dot(g_ref[:, columns], before, (1, 1)),
                trailing * dot(v_ref[:, columns], later, (1, 1)),
                trailing * dot(k_ref[:, columns], later, (1, 0)),
            )
            start = pl.multiple_of((base + s * together) * DH, DH)
            for n, part in enumerate(parts):
                scratch[n, :, columns] = (inside_ref[n, :, columns] + part).astype(BF16)
                copy = pltpu.make_async_copy(
                    scratch.at[n, :, columns], outs[n].at[:, pl.ds(start, together * DH)], sems.at[s, n]
                )
                copy.start()
                copies.append(copy)
        for copy in copies:
            copy.wait()

    vmem = pl.BlockSpec(memory_space=pltpu.VMEM)
    hbm = pl.BlockSpec(memory_space=pltpu.HBM)
    return pl.pallas_call(
        body,
        in_specs=[pl.BlockSpec(memory_space=pltpu.SMEM)] + [vmem] * 5 + [hbm] * len(previous),
        out_specs=[hbm] * 3,
        out_shape=[jax.ShapeDtypeStruct((rows, width), BF16)] * 3,
        scratch_shapes=[pltpu.VMEM((3, rows, count * DH), BF16), pltpu.SemaphoreType.DMA((steps, 3))],
        input_output_aliases={6 + i: i for i in range(len(previous))},
        cost_estimate=pl.CostEstimate(
            flops=count * 6 * rows * DH * DH, bytes_accessed=count * rows * DH * 6, transcendentals=0
        ),
        compiler_params=pltpu.CompilerParams(vmem_limit_bytes=8 << 20),
        name="across_blocks",
    )(rates, *staged[1:], inside, carries, *previous)


def steps_of(count, first):
    return next(n for n in (4, 3, 2, 1) if count % n == 0 and first % n == 0)


def local(shape, query, key, value, grad, rates):
    rows = query.shape[0]
    heads = query.shape[1] // DH
    group = shape["head"]
    depth = shape["ctx"] // 2
    bits = (depth - 1).bit_length()
    units = heads // (2 * group)
    sizes = [(units + CHUNKS - 1 - n) // CHUNKS for n in range(CHUNKS)]
    chunks, first = [], 0
    for per in sizes:
        if per:
            chunks.append((first, per * group, per))
            first += 2 * per * group
    arrays = tuple(pltpu.with_memory_space_constraint(a, pltpu.HBM) for a in (query, key, value, grad))

    def load(chunk, mine, done):
        first, count, per = chunk
        step = steps_of(count, first)
        return block_states(
            shape, first, count, step, mine, F32 if mine else BF16, after(rates, *done), *arrays
        )

    def down(chunk, done):
        first, count, per = chunk
        staged_other, send = load(chunk, False, done)
        other = exchange(send, shape, "core", 1)
        staged_own, own = load(chunk, True, (send,))
        keep, *sends = chip_totals(shape, rows, first, count, group, per, rates, own, other)
        others = [exchange(s, shape, "group", f + 1) for f, s in enumerate(sends)]
        return dict(own=own, other=other, keep=keep, others=others, staged=(staged_own, staged_other))

    def across(chunk, c, done):
        first, count, per = chunk
        sends = group_totals(shape, rows, first, count, group, per, bits, after(rates, *done), c["keep"], c["others"])
        c["zs"] = [exchange(sends[f.bit_length() - 1], shape, "z", f) for f in range(1, depth)]
        return sends[0]

    def up(chunk, c, done):
        first, count, per = chunk
        mine, *sends = group_carries(
            shape, rows, first, count, group, per, depth, after(rates, *done), c["keep"], c["others"], c["zs"]
        )
        c["carries"] = [mine] + [exchange(s, shape, "group", f + 1) for f, s in enumerate(sends)]
        return mine

    def inside(chunk, c, mine, done):
        first, count, per = chunk
        part = within_block(shape, first, count, mine, after(rates, *done), c["staged"][0 if mine else 1])
        c["own_part" if mine else "other_part"] = part
        return part

    def finish(chunk, c, outs, done):
        first, count, per = chunk
        state, send = device_carries(
            shape, rows, first, count, group, per, after(rates, *done), c["own"], c["other"], c["carries"]
        )
        other_state = exchange(send, shape, "core", 1)
        width = query.shape[1]
        outs = across_blocks(shape, first, count, True, width, rates, c["staged"][0], c["own_part"], state, outs)
        return across_blocks(
            shape, first, count, False, width, rates, c["staged"][1], c["other_part"], other_state, outs
        )

    kept, last = [], ()
    for chunk in chunks:
        kept.append(down(chunk, last))
        last = (kept[-1]["keep"],)
    pairs = list(zip(chunks, kept))
    for chunk, c in pairs:
        last = (across(chunk, c, last),)
        last = (inside(chunk, c, True, last),)
    for chunk, c in pairs:
        last = (up(chunk, c, last),)
        last = (inside(chunk, c, False, last),)
    outs = ()
    for chunk, c in pairs:
        outs = finish(chunk, c, outs, last)
        last = (outs[0],)
    return tuple(outs)


def solution(mesh):
    split = P(AXES, None)
    return jax.shard_map(
        functools.partial(local, dict(mesh.shape)),
        mesh=mesh,
        in_specs=(split, split, split, split, P()),
        out_specs=(split, split, split),
        check_vma=False,
    )
```

```python
import jax
import jax.numpy as jnp
from jax import lax
from jax.experimental import pallas as pl
from jax.experimental.pallas import tpu as pltpu
from jax.sharding import PartitionSpec as P

DH = 128
AXES = ("ctx", "head")
CHUNKS = 2

F32 = jnp.float32
BF16 = jnp.bfloat16


def dot(a, b, contract):
    return lax.dot_general(a, b, ((contract[:1], contract[1:]), ((), ())), preferred_element_type=F32)


def splat(rate, count):
    return jnp.exp(jnp.full((8, DH), -rate * count, F32))


def scaled(weight, state):
    return (state.astype(F32).reshape(DH // 8, 8, DH) * weight[None]).reshape(DH, DH)


def place(shape):
    ctx, head = lax.axis_index("ctx"), lax.axis_index("head")
    ys = shape["head"] // 2
    return head % 2, (ctx % 2) * ys + head // 2, ctx // 2


def exchange(value, shape, level, flip):
    ys = shape["head"] // 2
    pairs = []
    for source in range(shape["ctx"] * shape["head"]):
        ctx, head = divmod(source, shape["head"])
        core, member, z = head % 2, (ctx % 2) * ys + head // 2, ctx // 2
        if level == "core":
            core ^= flip
        elif level == "group":
            member ^= flip
        else:
            z ^= flip
        target = ((z * 2 + member // ys) * ys + member % ys) * 2 + core
        pairs.append((source, target))
    return lax.ppermute(value, AXES, pairs)


def first_head(shape, first, count, mine):
    core = place(shape)[0]
    return first + (core if mine else 1 - core) * count


def after(value, *done):
    return lax.optimization_barrier((value, done))[0]


def block_states(shape, first, count, per_step, mine, dtype, rates, *arrays):
    rows = arrays[0].shape[0]
    steps = count // per_step
    width = per_step * DH

    def body(rates_ref, *refs):
        sources, staged, out_ref, sems = refs[:4], refs[4:8], refs[8], refs[9]
        base = first_head(shape, first, count, mine)
        copies = []
        for s in range(steps):
            start = pl.multiple_of((base + s * per_step) * DH, DH)
            copies.append([
                pltpu.make_async_copy(
                    source.at[:, pl.ds(start, width)], stage.at[:, pl.ds(s * width, width)], sems.at[s, n]
                )
                for n, (source, stage) in enumerate(zip(sources, staged))
            ])
        for group in copies:
            for copy in group:
                copy.start()
        position = lax.broadcasted_iota(jnp.int32, (1, rows), 1).astype(F32)
        q_ref, k_ref, v_ref, g_ref = staged
        for s in range(steps):
            for copy in copies[s]:
                copy.wait()
            for i in range(s * per_step, (s + 1) * per_step):
                rate = rates_ref[base + i]
                columns = slice(i * DH, (i + 1) * DH)
                key_decay = jnp.exp(-rate * (rows - 1.0 - position))
                query_decay = jnp.exp(-rate * position)
                keys = (k_ref[:, columns].T.astype(F32) * key_decay).astype(BF16)
                queries = (q_ref[:, columns].T.astype(F32) * query_decay).astype(BF16)
                out_ref[0, i] = dot(keys, v_ref[:, columns], (1, 0)).astype(dtype)
                out_ref[1, i] = dot(queries, g_ref[:, columns], (1, 0)).astype(dtype)

    vmem = pl.BlockSpec(memory_space=pltpu.VMEM)
    out = pl.pallas_call(
        body,
        in_specs=[pl.BlockSpec(memory_space=pltpu.SMEM)] + [pl.BlockSpec(memory_space=pltpu.HBM)] * 4,
        out_specs=[vmem] * 5,
        out_shape=[jax.ShapeDtypeStruct((rows, count * DH), BF16)] * 4 + [states(count, dtype)],
        scratch_shapes=[pltpu.SemaphoreType.DMA((steps, 4))],
        cost_estimate=pl.CostEstimate(
            flops=count * 4 * rows * DH * DH, bytes_accessed=count * rows * DH * 8, transcendentals=0
        ),
        compiler_params=pltpu.CompilerParams(vmem_limit_bytes=8 << 20),
        name="block_states",
    )(rates, *arrays)
    return out[:4], out[4]


def whole_call(body, outs, *args, flops=0, scratch=()):
    vmem = pl.BlockSpec(memory_space=pltpu.VMEM)
    size = sum(a.size * a.dtype.itemsize for a in args) + sum(o.size * o.dtype.itemsize for o in outs)
    return pl.pallas_call(
        body,
        in_specs=[pl.BlockSpec(memory_space=pltpu.SMEM)] + [vmem] * (len(args) - 1),
        out_specs=[vmem] * len(outs),
        out_shape=outs,
        scratch_shapes=scratch,
        cost_estimate=pl.CostEstimate(flops=flops, bytes_accessed=size, transcendentals=0),
        compiler_params=pltpu.CompilerParams(vmem_limit_bytes=8 << 20),
    )(*args)


def states(heads, dtype, lead=(2,)):
    return jax.ShapeDtypeStruct((*lead, heads, DH, DH), dtype)


def chip_totals(shape, rows, first, count, group, per, rates, own, other):
    def body(rates_ref, own_ref, other_ref, keep_ref, *send_refs):
        core, member, _ = place(shape)
        base = first + core * count
        for flip in range(group):
            start = (member ^ flip) * per
            for i in range(per):
                rate = rates_ref[base + start + i]
                early = splat(rate, rows * (1 - core).astype(F32))
                late = splat(rate, rows * core.astype(F32))
                total = scaled(early, own_ref[0, start + i]) + scaled(late, other_ref[0, start + i])
                after = scaled(late, own_ref[1, start + i]) + scaled(early, other_ref[1, start + i])
                out = keep_ref if flip == 0 else send_refs[flip - 1]
                out[0, i] = total.astype(out.dtype)
                out[1, i] = after.astype(out.dtype)

    outs = [states(per, F32)] + [states(per, BF16)] * (group - 1)
    return whole_call(body, outs, rates, own, other)


def group_totals(shape, rows, first, count, group, per, bits, rates, keep, others):
    def body(rates_ref, keep_ref, *refs):
        other_refs, send_refs = refs[: group - 1], refs[group - 1 :]
        core, member, z = place(shape)
        base = first + core * count + member * per
        for i in range(per):
            rate = rates_ref[base + i]
            total = after = jnp.zeros((DH, DH), F32)
            for flip in range(group):
                ref = keep_ref if flip == 0 else other_refs[flip - 1]
                where = member ^ flip
                total += scaled(splat(rate, 2.0 * rows * (group - 1 - where).astype(F32)), ref[0, i])
                after += scaled(splat(rate, 2.0 * rows * where.astype(F32)), ref[1, i])
            for bit in range(bits):
                lower = (z >> bit) % 2 == 0
                send_refs[bit][i] = jnp.where(lower, total, after).astype(BF16)

    return whole_call(body, [states(per, BF16, ())] * bits, rates, keep, *others)


def group_carries(shape, rows, first, count, group, per, depth, rates, keep, others, zs):
    def body(rates_ref, keep_ref, *refs):
        other_refs, z_refs = refs[: group - 1], refs[group - 1 : group + depth - 2]
        own_ref, *send_refs = refs[group + depth - 2 :]
        core, member, z = place(shape)
        base = first + core * count + member * per

        def weight(rate, span, steps):
            kept = jnp.where(steps >= 0, 1.0, 0.0)
            return splat(rate, span * jnp.maximum(steps, 0).astype(F32)) * kept

        for i in range(per):
            rate = rates_ref[base + i]
            before = after = jnp.zeros((DH, DH), F32)
            for flip in range(1, depth):
                where = z ^ flip
                before += scaled(weight(rate, 2.0 * group * rows, z - 1 - where), z_refs[flip - 1][i])
                after += scaled(weight(rate, 2.0 * group * rows, where - z - 1), z_refs[flip - 1][i])
            for target in range(group):
                at = member ^ target
                here = scaled(splat(rate, 2.0 * rows * at.astype(F32)), before)
                there = scaled(splat(rate, 2.0 * rows * (group - 1 - at).astype(F32)), after)
                for flip in range(group):
                    ref = keep_ref if flip == 0 else other_refs[flip - 1]
                    where = member ^ flip
                    here += scaled(weight(rate, 2.0 * rows, at - 1 - where), ref[0, i])
                    there += scaled(weight(rate, 2.0 * rows, where - at - 1), ref[1, i])
                out = own_ref if target == 0 else send_refs[target - 1]
                out[0, i] = here.astype(out.dtype)
                out[1, i] = there.astype(out.dtype)

    outs = [states(per, F32)] + [states(per, BF16)] * (group - 1)
    return whole_call(body, outs, rates, keep, *others, *zs)


def device_carries(shape, rows, first, count, group, per, rates, own, other, carries):
    def body(rates_ref, own_ref, other_ref, *refs):
        carry_refs, (mine_ref, send_ref) = refs[:group], refs[group:]
        core, member, _ = place(shape)
        base = first + core * count
        zero_first = (core == 0).astype(F32)
        for flip in range(group):
            start = (member ^ flip) * per
            for i in range(per):
                at = start + i
                rate = rates_ref[base + at]
                before = carry_refs[flip][0, i].astype(F32)
                after = carry_refs[flip][1, i].astype(F32)
                early = splat(rate, rows * (1.0 - zero_first))
                late = splat(rate, rows * zero_first)
                mine_ref[0, at] = (scaled(early, before) + (1.0 - zero_first) * other_ref[0, at].astype(F32)).astype(BF16)
                mine_ref[1, at] = (scaled(late, after) + zero_first * other_ref[1, at].astype(F32)).astype(BF16)
                send_ref[0, at] = (scaled(late, before) + zero_first * own_ref[0, at].astype(F32)).astype(BF16)
                send_ref[1, at] = (scaled(early, after) + (1.0 - zero_first) * own_ref[1, at].astype(F32)).astype(BF16)

    return whole_call(body, [states(count, BF16)] * 2, rates, own, other, *carries)


def sublane_powers(rate, rows, sign):
    position = lax.broadcasted_iota(jnp.int32, (8, DH), 0).astype(F32)
    powers = jnp.exp(sign * rate * position)
    size = 8
    while size < rows:
        powers = jnp.concatenate([powers, jnp.tile(splat(rate, -sign * size), (size // 8, 1)) * powers], axis=0)
        size *= 2
    return powers


def within_block(shape, first, count, mine, rates, staged):
    rows = staged[0].shape[0]
    blocks = rows // DH
    spans = [(slice(a * DH, (a + 1) * DH), slice(a * DH, rows)) for a in range(blocks)]

    def weigh(rate, q, k, v, g, held):
        lane = lax.broadcasted_iota(jnp.int32, (1, DH), 1).astype(F32)
        row_index = lax.broadcasted_iota(jnp.int32, (DH, DH), 0)
        column_index = lax.broadcasted_iota(jnp.int32, (DH, DH), 1)
        full = sublane_powers(rate, DH, 1.0) * jnp.exp(-rate * lane)
        masks = [jnp.where(row_index <= column_index, full, 0.0)]
        for n in range(1, blocks):
            masks.append(full * jnp.tile(splat(rate, float(n * DH)), (DH // 8, 1)))
        for a, (here, rest) in enumerate(spans):
            mask = jnp.concatenate(masks[: blocks - a], axis=1)
            held[0, here, rest] = (dot(v[here], g[rest], (1, 1)) * mask).astype(BF16)
            held[1, here, rest] = (dot(k[here], q[rest], (1, 1)) * mask).astype(BF16)

    def apply(q, k, g, held, put):
        for b, (here, rest) in enumerate(spans):
            put(1, here, dot(held[0, here, rest], q[rest], (1, 0)))
            put(2, here, dot(held[1, here, rest], g[rest], (1, 0)))
            pieces = [held[0, spans[a][0], here].T for a in range(b + 1)]
            put(0, here, dot(jnp.concatenate(pieces, axis=1), k[: (b + 1) * DH], (1, 0)))

    def body(rates_ref, q_ref, k_ref, v_ref, g_ref, out_ref, *held):
        base = first_head(shape, first, count, mine)

        def columns(head):
            return pl.ds(pl.multiple_of(head * DH, DH), DH)

        def weigh_head(head, slot):
            weigh(rates_ref[base + head], *(ref.at[:, columns(head)] for ref in (q_ref, k_ref, v_ref, g_ref)), held[slot])

        def apply_head(head, slot):
            def put(n, here, block):
                out_ref[n, here, columns(head)] = block

            apply(*(ref.at[:, columns(head)] for ref in (q_ref, k_ref, g_ref)), held[slot], put)

        weigh_head(0, 0)

        def step(s, carry):
            weigh_head(2 * s + 1, 1)
            apply_head(2 * s, 0)
            weigh_head(jnp.minimum(2 * s + 2, count - 1), 0)
            apply_head(2 * s + 1, 1)
            return carry

        lax.fori_loop(0, count // 2, step, 0)

    return whole_call(
        body, [jax.ShapeDtypeStruct((3, rows, count * DH), F32)], rates, *staged,
        flops=count * 13 * rows * rows * DH // 2, scratch=[pltpu.VMEM((2, rows, rows), BF16)] * 2,
    )[0]


def across_blocks(shape, first, count, mine, width, rates, staged, inside, carries, previous):
    rows = staged[0].shape[0]
    together = 2 if count % 2 == 0 else 1
    steps = count // together

    def diagonal(pair):
        if len(pair) == 1:
            return pair[0]
        zero = jnp.zeros((DH, DH), BF16)
        return jnp.concatenate(
            [jnp.concatenate([pair[0], zero], axis=1), jnp.concatenate([zero, pair[1]], axis=1)], axis=0
        )

    def body(rates_ref, k_ref, v_ref, g_ref, inside_ref, carry_ref, *refs):
        outs, scratch, sems = refs[-5:-2], refs[-2], refs[-1]
        base = first_head(shape, first, count, mine)
        copies = []
        for s in range(steps):
            heads = range(s * together, (s + 1) * together)
            columns = slice(s * together * DH, (s + 1) * together * DH)
            rates_here = [rates_ref[base + h] for h in heads]
            leading = jnp.concatenate(
                [sublane_powers(r, rows, -1.0) * jnp.tile(splat(r, 1.0), (rows // 8, 1)) for r in rates_here], axis=1
            )
            trailing = jnp.concatenate(
                [sublane_powers(r, rows, 1.0) * jnp.tile(splat(r, float(rows)), (rows // 8, 1)) for r in rates_here],
                axis=1,
            )
            before = diagonal([carry_ref[0, h] for h in heads])
            later = diagonal([carry_ref[1, h] for h in heads])
            parts = (
                leading * dot(g_ref[:, columns], before, (1, 1)),
                trailing * dot(v_ref[:, columns], later, (1, 1)),
                trailing * dot(k_ref[:, columns], later, (1, 0)),
            )
            start = pl.multiple_of((base + s * together) * DH, DH)
            for n, part in enumerate(parts):
                scratch[n, :, columns] = (inside_ref[n, :, columns] + part).astype(BF16)
                copy = pltpu.make_async_copy(
                    scratch.at[n, :, columns], outs[n].at[:, pl.ds(start, together * DH)], sems.at[s, n]
                )
                copy.start()
                copies.append(copy)
        for copy in copies:
            copy.wait()

    vmem = pl.BlockSpec(memory_space=pltpu.VMEM)
    hbm = pl.BlockSpec(memory_space=pltpu.HBM)
    return pl.pallas_call(
        body,
        in_specs=[pl.BlockSpec(memory_space=pltpu.SMEM)] + [vmem] * 5 + [hbm] * len(previous),
        out_specs=[hbm] * 3,
        out_shape=[jax.ShapeDtypeStruct((rows, width), BF16)] * 3,
        scratch_shapes=[pltpu.VMEM((3, rows, count * DH), BF16), pltpu.SemaphoreType.DMA((steps, 3))],
        input_output_aliases={6 + i: i for i in range(len(previous))},
        cost_estimate=pl.CostEstimate(
            flops=count * 6 * rows * DH * DH, bytes_accessed=count * rows * DH * 6, transcendentals=0
        ),
        compiler_params=pltpu.CompilerParams(vmem_limit_bytes=8 << 20),
        name="across_blocks",
    )(rates, *staged[1:], inside, carries, *previous)


def steps_of(count, first):
    return next(n for n in (4, 3, 2, 1) if count % n == 0 and first % n == 0)


def local(shape, query, key, value, grad, rates):
    rows = query.shape[0]
    heads = query.shape[1] // DH
    group = shape["head"]
    depth = shape["ctx"] // 2
    bits = (depth - 1).bit_length()
    units = heads // (2 * group)
    sizes = [(units + CHUNKS - 1 - n) // CHUNKS for n in range(CHUNKS)]
    chunks, first = [], 0
    for per in sizes:
        if per:
            chunks.append((first, per * group, per))
            first += 2 * per * group
    arrays = tuple(pltpu.with_memory_space_constraint(a, pltpu.HBM) for a in (query, key, value, grad))

    def load(chunk, mine, done):
        first, count, _ = chunk
        step = steps_of(count, first)
        return block_states(
            shape, first, count, step, mine, F32 if mine else BF16, after(rates, *done), *arrays
        )

    def down(chunk, done):
        first, count, per = chunk
        staged_other, send = load(chunk, False, done)
        other = exchange(send, shape, "core", 1)
        staged_own, own = load(chunk, True, (send,))
        keep, *sends = chip_totals(shape, rows, first, count, group, per, rates, own, other)
        others = [exchange(s, shape, "group", f + 1) for f, s in enumerate(sends)]
        return dict(own=own, other=other, keep=keep, others=others, staged=(staged_own, staged_other))

    def across(chunk, c, done):
        first, count, per = chunk
        sends = group_totals(shape, rows, first, count, group, per, bits, after(rates, *done), c["keep"], c["others"])
        c["zs"] = [exchange(sends[f.bit_length() - 1], shape, "z", f) for f in range(1, depth)]
        return sends[0]

    def up(chunk, c, done):
        first, count, per = chunk
        mine, *sends = group_carries(
            shape, rows, first, count, group, per, depth, after(rates, *done), c["keep"], c["others"], c["zs"]
        )
        c["carries"] = [mine] + [exchange(s, shape, "group", f + 1) for f, s in enumerate(sends)]
        return mine

    def inside(chunk, c, mine, done):
        first, count, _ = chunk
        part = within_block(shape, first, count, mine, after(rates, *done), c["staged"][0 if mine else 1])
        c["own_part" if mine else "other_part"] = part
        return part

    def finish(chunk, c, outs, done):
        first, count, per = chunk
        state, send = device_carries(
            shape, rows, first, count, group, per, after(rates, *done), c["own"], c["other"], c["carries"]
        )
        other_state = exchange(send, shape, "core", 1)
        width = query.shape[1]
        outs = across_blocks(shape, first, count, True, width, rates, c["staged"][0], c["own_part"], state, outs)
        return across_blocks(
            shape, first, count, False, width, rates, c["staged"][1], c["other_part"], other_state, outs
        )

    kept, last = {}, ()
    chunks = dict(zip("abcdefgh", chunks))
    for name, chunk in chunks.items():
        kept[name] = down(chunk, last)
        last = (kept[name]["keep"],)
    for name, chunk in chunks.items():
        last = (across(chunk, kept[name], last),)
        last = (inside(chunk, kept[name], True, last),)
    for name, chunk in chunks.items():
        last = (up(chunk, kept[name], last),)
        last = (inside(chunk, kept[name], False, last),)
    outs = ()
    for name, chunk in chunks.items():
        outs = finish(chunk, kept[name], outs, last)
        last = (outs[0],)
    return tuple(outs)


def solution(mesh):
    split = P(AXES, None)
    shape = dict(mesh.shape)

    def step(*args):
        return local(shape, *args)

    return jax.shard_map(
        step,
        mesh=mesh,
        in_specs=(split, split, split, split, P()),
        out_specs=(split, split, split),
        check_vma=False,
    )
```
